32 devices in a mesh: layer: 8 (over z, y), group: 4 (over x, core).
Axes of the slice: x: 2, y: 2, z: 4, core: 2. Of those that a mesh axis runs over, the one named last changes fastest.
Arguments:
- travelling_layer_entries: float32 [8, 4, 1024, 256], P('layer', 'group'), may hold values from -6 to 6
- arriving_clusters: float32 [4, 8, 1024, 256], P('group'), may hold values from -6 to 6
- travelling_cluster_position: int32 [8, 4], replicated, may hold values from 0 to 1
- arriving_cluster_position: int32 [4, 8], replicated, may hold values from 0 to 1
- adjacency_patches: bfloat16 [8, 48, 128, 128], P('group'), may hold values from -0.21875 to 0.21875
- patch_read_range: int32 [8, 48], P('group'), may hold values from 0 to 63
- patch_write_range: int32 [8, 48], P('group'), may hold values from 0 to 7
- outdated_layer_entries: bfloat16 [8, 8192, 256], P('layer'), may hold values from -6 to 6
- neighbour_mixing_matrix: bfloat16 [8, 256, 256], P('layer'), may hold values from -0.375 to 0.375
- rescale_factors: float32 [8, 256], P('layer'), may hold values from 0.5 to 1.5
- expand_matrix: bfloat16 [8, 256, 512], P('layer'), may hold values from -0.375 to 0.375
- contract_matrix: bfloat16 [8, 512, 256], P('layer'), may hold values from -0.25 to 0.25
Outputs:
- outputs: float32 [8, 4, 1024, 256], P('layer', 'group')
- history_out: bfloat16 [8, 8192, 256], P('layer')
The draws below stay inside these ranges and needn't reach their ends.
Inputs may be any that keep to these rules, and one draw needn't show every extreme that they name: `travelling_cluster_position`: local slot of a group within its stream. `arriving_cluster_position`: local slot of a new group within its stream. `patch_read_range`: row block of a layer's whole history.
All inputs are finite; a program needn't handle non-finite values.
Results may differ from the reference program's by a relative error of at most 0.0095.
Values may be sent and summed in bfloat16 or wider, within the bound.
A program may use at most 128 MiB of HBM per device.

```python
import jax
import jax.numpy as jnp
from jax import lax

EMBED_BREADTH = 256
FF = 512
TB = 128
TILES = 48
STREAM_SLOTS = 2
CLUSTER_NODES = 1024
RELAY_BEATS = 8
NETWORK_DEPTH = 8
SLOTS = 8
HIST = 8192
BLOCKS = 64
NB = 8
N_GROUP = 4


def plant(values, own_key, low, top_value):
    longest = values.shape.index(max(values.shape))
    spots = []
    for shift in (0, 1):
        where = [jax.random.randint(jax.random.fold_in(own_key, axis), (), 0, length) for axis, length in enumerate(values.shape)]
        where[longest] = (where[longest] + shift) % values.shape[longest]
        spots.append(tuple(where))
    return values.at[spots[0]].set(low).at[spots[1]].set(top_value)


def levels(own_key, extent, shards, least, largest):
    def one(axis_at, parts):
        steps = jax.random.uniform(jax.random.fold_in(jax.random.fold_in(own_key, 6), axis_at), (parts,), jnp.float32, least / len(shards), largest / len(shards))
        return jnp.repeat(jnp.exp(steps), extent[axis_at] // parts).reshape((-1,) + (1,) * (len(extent) - axis_at - 1))

    loudness = one(*shards[0])
    for cut in shards[1:]:
        loudness = loudness * one(*cut)
    return loudness


def normal_values(key, shape, scale, limit, cuts=(), kind=jnp.bfloat16):
    loudness = levels(key, shape, cuts, -0.22, 0.18) if cuts else 1.0
    entries = jax.random.normal(key, shape, jnp.float32) * scale * loudness
    return jnp.minimum(jnp.maximum(entries, -limit), limit).astype(kind)


def setup_inputs(seed: int = 0) -> dict:
    streams_of = jax.random.split(jax.random.key(seed), 13)
    return {
        "travelling_layer_entries": normal_values(streams_of[0], (NETWORK_DEPTH, N_GROUP, CLUSTER_NODES, EMBED_BREADTH), 1.0, 6.0, ((0, 8), (1, 4)), jnp.float32),
        "arriving_clusters": normal_values(streams_of[1], (N_GROUP, RELAY_BEATS, CLUSTER_NODES, EMBED_BREADTH), 1.0, 6.0, ((0, 4),), jnp.float32),
        "travelling_cluster_position": plant(jax.random.randint(streams_of[2], (NETWORK_DEPTH, N_GROUP), 0, STREAM_SLOTS), jax.random.fold_in(streams_of[2], 1), 0, STREAM_SLOTS - 1).astype(jnp.int32),
        "arriving_cluster_position": plant(jax.random.randint(streams_of[3], (N_GROUP, RELAY_BEATS), 0, STREAM_SLOTS), jax.random.fold_in(streams_of[3], 1), 0, STREAM_SLOTS - 1).astype(jnp.int32),
        "adjacency_patches": normal_values(streams_of[4], (SLOTS, TILES, TB, TB), (TILES * TB * TB // CLUSTER_NODES) ** -0.5, 0.21875, ((0, 4),)),
        "patch_read_range": plant(jax.random.randint(streams_of[5], (SLOTS, TILES), 0, BLOCKS), jax.random.fold_in(streams_of[5], 1), 0, BLOCKS - 1).astype(jnp.int32),
        "patch_write_range": plant(jax.random.randint(streams_of[6], (SLOTS, TILES), 0, NB), jax.random.fold_in(streams_of[6], 1), 0, NB - 1).astype(jnp.int32),
        "outdated_layer_entries": normal_values(streams_of[7], (NETWORK_DEPTH, HIST, EMBED_BREADTH), 1.0, 6.0, ((0, 8),)),
        "neighbour_mixing_matrix": normal_values(streams_of[8], (NETWORK_DEPTH, EMBED_BREADTH, EMBED_BREADTH), EMBED_BREADTH ** -0.5, 0.375, ((0, 8),)),
        "rescale_factors": jnp.clip(0.5 + 1.0 * jax.random.uniform(streams_of[9], (NETWORK_DEPTH, EMBED_BREADTH), jnp.float32) ** levels(streams_of[9], (NETWORK_DEPTH, EMBED_BREADTH), ((0, 8),), -0.2, 0.2), 0.5, 1.5),
        "expand_matrix": normal_values(streams_of[10], (NETWORK_DEPTH, EMBED_BREADTH, FF), EMBED_BREADTH ** -0.5, 0.375, ((0, 8),)),
        "contract_matrix": normal_values(streams_of[11], (NETWORK_DEPTH, FF, EMBED_BREADTH), FF ** -0.5, 0.25, ((0, 8),)),
    }


def layer_rows(inputs, aggregated, conv_mat, norm_vec, up_mat, down_mat):
    convolved = jnp.dot(aggregated, conv_mat, preferred_element_type=jnp.float32)
    residual_sum = inputs + jax.nn.relu(convolved)
    scale = lax.rsqrt(lax.optimization_barrier(jnp.mean(residual_sum * residual_sum, axis=-1, keepdims=True)) + 1e-06)
    normed = (residual_sum * scale * norm_vec).astype(jnp.bfloat16)
    hidden = jax.nn.gelu(jnp.dot(normed, up_mat, preferred_element_type=jnp.float32)).astype(jnp.bfloat16)
    return residual_sum + jnp.dot(hidden, down_mat, preferred_element_type=jnp.float32)

def aggregate(history_now, tile_set, tile_from, tile_to):
    blocks = history_now.reshape(-1, TB, history_now.shape[-1])[tile_from]
    products = jnp.einsum('tij,tjd->tid', tile_set.astype(jnp.float32), blocks.astype(jnp.float32), precision=lax.Precision.HIGHEST)
    onehot = (tile_to[None, :] == jnp.arange(CLUSTER_NODES // TB, dtype=jnp.int32)[:, None]).astype(jnp.float32)
    summed = jnp.einsum('bt,tid->bid', onehot, products, precision=lax.Precision.HIGHEST)
    return summed.reshape(CLUSTER_NODES, -1).astype(jnp.bfloat16)

def reference(travelling_layer_entries, arriving_clusters, travelling_cluster_position, arriving_cluster_position, adjacency_patches, patch_read_range, patch_write_range, outdated_layer_entries, neighbour_mixing_matrix, rescale_factors, expand_matrix, contract_matrix):
    cluster_response_entries = travelling_layer_entries
    slot_lookup_table = travelling_cluster_position
    history_all = outdated_layer_entries

    def one_layer(packed):
        acts, history_slot_list, history_now, conv_mat, norm_vec, up_mat, down_mat = packed
        written = acts.astype(jnp.bfloat16)
        for group_stream in range(N_GROUP):
            global_slot_index = (group_stream * STREAM_SLOTS + history_slot_list[group_stream]).astype(jnp.int32)
            history_now = lax.dynamic_update_slice(history_now, written[group_stream], ((global_slot_index * CLUSTER_NODES).astype(jnp.int32), jnp.int32(0)))
        results = []
        for group_stream in range(N_GROUP):
            global_slot_index = (group_stream * STREAM_SLOTS + history_slot_list[group_stream]).astype(jnp.int32)
            aggregated = aggregate(history_now, adjacency_patches[global_slot_index], patch_read_range[global_slot_index], patch_write_range[global_slot_index])
            results.append(layer_rows(acts[group_stream], aggregated, conv_mat, norm_vec, up_mat, down_mat))
        return (jnp.stack(results), history_now)
    results = cluster_response_entries
    for beat_no in range(RELAY_BEATS):
        results, history_all = lax.map(one_layer, (cluster_response_entries, slot_lookup_table, history_all, neighbour_mixing_matrix, rescale_factors, expand_matrix, contract_matrix))
        if beat_no < RELAY_BEATS - 1:
            cluster_response_entries = jnp.concatenate([arriving_clusters[:, beat_no][None], results[:-1]], axis=0)
            slot_lookup_table = jnp.concatenate([arriving_cluster_position[:, beat_no][None], slot_lookup_table[:-1]], axis=0)
    return (results, history_all)
```

```python
import functools

import jax
import jax.numpy as jnp
from jax import lax
from jax.experimental import pallas as pl
from jax.experimental.pallas import tpu as pltpu
from jax.sharding import PartitionSpec as P

MESH = pl.DeviceIdType.MESH
CHUNKS = 4
UNROLL = 4


def pair_count(tiles, nb):
    pairs = (tiles + nb) // 2
    return -(-pairs // UNROLL) * UNROLL


def kernel(
    layers, streams, per_stream, beats, rows, tb, pairs,
    a_idx, b_row, keep, last, final_row,
    act_ref, feed_ref, tile_ref, hist_ref, mix_ref, gain_ref, up_ref, down_ref,
    out_ref, hist_out,
    hist, tiles, land, stage, segs, sbuf,
    local_sem, hist_sem, tile_sem, y_send, y_recv, sib_send, sib_recv, x_send, x_recv, r_send, r_recv,
):
    layer = lax.axis_index("layer")
    me = lax.axis_index("group")
    core = lax.rem(me, 2)
    sib = me + 1 - 2 * core
    cross = lax.rem(me + 2, streams)
    cross_sib = cross + 1 - 2 * core
    crows = rows // CHUNKS
    nb = rows // tb
    slots = streams * per_stream
    first_layer = layer == 0
    last_layer = layer == layers - 1

    old = pltpu.make_async_copy(hist_ref, hist.at[pl.ds(0, slots * nb)], hist_sem)
    old.start()
    load = pltpu.make_async_copy(tile_ref, tiles.at[pl.ds(0, tile_ref.shape[0])], tile_sem)
    load.start()
    tiles[tile_ref.shape[0]] = jnp.zeros((tb, tb), jnp.bfloat16)
    segs[pairs] = jnp.zeros((tb, hist.shape[2]), jnp.bfloat16)

    barrier = pltpu.get_barrier_semaphore()
    for peer in (sib, cross):
        pl.semaphore_signal(barrier, inc=1, device_id={"group": peer}, device_id_type=MESH)

    @pl.when(layer > 0)
    def _():
        pl.semaphore_signal(barrier, inc=1, device_id={"layer": layer - 1}, device_id_type=MESH)

    @pl.when(layer < layers - 1)
    def _():
        pl.semaphore_signal(barrier, inc=1, device_id={"layer": layer + 1}, device_id_type=MESH)

    inner = (layer > 0).astype(jnp.int32) + (layer < layers - 1).astype(jnp.int32)
    pl.semaphore_wait(barrier, 2 + inner)

    def piece(k):
        return pl.ds(pl.multiple_of(k * crows, crows), crows)

    def y_copy(b, k):
        return pltpu.make_async_remote_copy(
            src_ref=sbuf.at[piece(k)],
            dst_ref=land.at[b, me, piece(k)],
            send_sem=y_send.at[k],
            recv_sem=y_recv.at[b, k],
            device_id={"layer": layer + 1},
            device_id_type=MESH,
        )

    def group_copy(b, k, stream, send, recv, to):
        return pltpu.make_async_remote_copy(
            src_ref=land.at[b, stream, piece(k)],
            dst_ref=land.at[b, stream, piece(k)],
            send_sem=send.at[k],
            recv_sem=recv.at[b, k],
            device_id={"group": to},
            device_id_type=MESH,
        )

    def keep_rows(b, stream, k):
        at = (slots + b * streams + stream) * nb + k * (crows // tb)
        for u in range(crows // tb):
            hist[at + u] = land[b, stream, pl.ds(k * crows + u * tb, tb), :]

    def beat(b, carry):
        source = jnp.logical_or(b == 0, first_layer)

        @pl.when(b == 0)
        def _():
            c = pltpu.make_async_copy(act_ref, stage, local_sem)
            c.start()
            c.wait()

        @pl.when(jnp.logical_and(b > 0, first_layer))
        def _():
            c = pltpu.make_async_copy(feed_ref.at[jnp.maximum(b - 1, 0)], stage, local_sem)
            c.start()
            c.wait()

        def cross_in(k):
            group_copy(b, k, cross, x_send, x_recv, cross).wait_recv()
            group_copy(b, k, cross, r_send, r_recv, sib).start()
            keep_rows(b, cross, k)

        for k in range(CHUNKS):
            @pl.when(source)
            def _():
                land[b, me, piece(k), :] = stage[piece(k), :].astype(jnp.bfloat16)

            @pl.when(jnp.logical_not(source))
            def _():
                y_copy(b, k).wait_recv()

            group_copy(b, k, me, x_send, x_recv, cross).start()
            group_copy(b, k, me, sib_send, sib_recv, sib).start()
            keep_rows(b, me, k)
            if k > 0:
                cross_in(k - 1)
        for k in range(CHUNKS):
            group_copy(b, k, sib, sib_send, sib_recv, sib).wait_recv()
            keep_rows(b, sib, k)
        cross_in(CHUNKS - 1)
        for k in range(CHUNKS):
            group_copy(b, k, cross_sib, r_send, r_recv, sib).wait_recv()
            keep_rows(b, cross_sib, k)

        @pl.when(b == 0)
        def _():
            old.wait()
            load.wait()

        def one_pair(q, total):
            def half(h):
                i = 2 * q + h
                return tiles[a_idx[b, i]], hist[b_row[b, i]]

            t0, b0 = half(0)
            t1, b1 = half(1)
            product = jnp.dot(
                jnp.concatenate([t0, t1], axis=1),
                jnp.concatenate([b0, b1], axis=0),
                preferred_element_type=jnp.float32,
            )
            total = total * keep[b, q] + product
            segs[q] = total.astype(jnp.bfloat16)
            return total

        def pair_step(s, total):
            for u in range(UNROLL):
                total = one_pair(s * UNROLL + u, total)
            return total

        width = hist.shape[2]
        lax.fori_loop(0, pairs // UNROLL, pair_step, jnp.zeros((tb, width), jnp.float32))

        def rows_step(k):
            blocks = []
            per = crows // tb
            for u in range(per):
                blocks.append(segs[last[b, k * per + u]])
            agg = jnp.concatenate(blocks, axis=0) if per > 1 else blocks[0]
            act = land[b, me, piece(k), :].astype(jnp.float32)
            mixed = act + jnp.maximum(
                jnp.dot(agg, mix_ref[...], preferred_element_type=jnp.float32), 0.0
            )
            scale = lax.rsqrt(jnp.mean(mixed * mixed, axis=-1, keepdims=True) + 1e-06)
            normed = (mixed * scale * gain_ref[...]).astype(jnp.bfloat16)
            hidden = jax.nn.gelu(
                jnp.dot(normed, up_ref[...], preferred_element_type=jnp.float32)
            ).astype(jnp.bfloat16)
            return mixed + jnp.dot(hidden, down_ref[...], preferred_element_type=jnp.float32)

        sends = jnp.logical_and(b < beats - 1, layer < layers - 1)
        for k in range(CHUNKS):
            @pl.when(jnp.logical_and(b > 0, layer < layers - 1))
            def _():
                y_copy(b, k).wait_send()

            res = rows_step(k)
            out_ref[piece(k), :] = res
            sbuf[piece(k), :] = res.astype(jnp.bfloat16)

            @pl.when(sends)
            def _():
                y_copy(b + 1, k).start()

        for k in range(CHUNKS):
            group_copy(b, k, me, x_send, x_recv, cross).wait_send()
            group_copy(b, k, me, sib_send, sib_recv, sib).wait_send()
            group_copy(b, k, cross, r_send, r_recv, sib).wait_send()
        return carry

    lax.fori_loop(0, beats, beat, 0)

    def final(i, carry):
        hist_out[i] = hist[final_row[0, i]]
        return carry

    lax.fori_loop(0, slots * nb, final, 0)


def tables(layer, me, tpos, apos, read, write, rows, tb):
    beats = apos.shape[1]
    streams = apos.shape[0]
    per_stream, tiles = read.shape
    nb = rows // tb
    slots = streams * per_stream
    pairs = pair_count(tiles, nb)
    i32 = jnp.int32
    seq = jnp.concatenate([apos.T[::-1], tpos], axis=0)
    slot = lax.dynamic_slice_in_dim(seq, layer + 1, beats, 0)[::-1]
    own = lax.dynamic_slice_in_dim(slot, me, 1, 1)[:, 0]
    bs = jnp.arange(beats, dtype=i32)
    js = jnp.arange(per_stream, dtype=i32)
    hit = (slot[None, :, :, None] == js) & (bs[None, :, None, None] <= bs[:, None, None, None])
    latest = jnp.max(jnp.where(hit, bs[None, :, None, None], -1), axis=1)
    cs = jnp.arange(streams, dtype=i32)
    cur = jnp.where(
        latest >= 0, slots + streams * latest + cs[None, :, None], cs[None, :, None] * per_stream + js
    ).reshape(beats, slots)
    ks = jnp.arange(nb, dtype=i32)
    ts = jnp.arange(tiles, dtype=i32)
    onto = write[:, :, None] == ks
    count = jnp.sum(onto.astype(i32), axis=1)
    half = (count + 1) // 2
    start = jnp.sum(jnp.where(ks[None, :, None] > ks[None, None, :], half[:, None, :], 0), axis=2)
    rank = jnp.sum(
        ((write[:, :, None] == write[:, None, :]) & (ts[None, None, :] < ts[None, :, None])).astype(i32),
        axis=2,
    )
    place = 2 * jnp.sum(jnp.where(onto, start[:, None, :], 0), axis=2) + rank
    qs = jnp.arange(2 * pairs, dtype=i32)
    at = place[:, None, :] == qs[None, :, None]
    ok = jnp.any(at, axis=2).astype(i32)
    tile = jnp.sum(jnp.where(at, ts, 0), axis=2) + jnp.where(ok > 0, js[:, None] * tiles, per_stream * tiles)
    block = jnp.sum(jnp.where(at, read[:, None, :], 0), axis=2)
    ps = jnp.arange(pairs, dtype=i32)
    resets = jnp.any((ps[None, :, None] == start[:, None, :]) & (half > 0)[:, None, :], axis=2)
    keep = 1.0 - resets.astype(jnp.float32)
    last = jnp.where(half > 0, start + half - 1, pairs)
    mine = own[:, None] == js

    def pick(x):
        return jnp.sum(jnp.where(mine[:, :, None], x[None], 0), axis=1)

    block_b = pick(block)
    ss = jnp.arange(slots, dtype=i32)
    base = jnp.sum(
        jnp.where((block_b // nb)[:, :, None] == ss, cur[:, None, :], 0), axis=2
    )
    b_row = base * nb + block_b % nb
    final_row = (cur[beats - 1][:, None] * nb + ks).reshape(1, slots * nb)
    return pick(tile), b_row, pick(keep), pick(last), final_row


def solution(mesh):
    layers = mesh.shape["layer"]
    streams = mesh.shape["group"]

    def local(act, feed, tpos, apos, tiles, read, write, hist, mix, gain, up, down):
        rows, width = act.shape[2:]
        per_stream, n_tiles, tb = tiles.shape[:3]
        beats = feed.shape[1]
        nb = rows // tb
        slots = streams * per_stream
        pairs = pair_count(n_tiles, nb)
        tabs = tables(
            lax.axis_index("layer"), lax.axis_index("group"), tpos, apos, read, write, rows, tb
        )
        smem = pl.BlockSpec(memory_space=pltpu.SMEM)
        vmem = pl.BlockSpec(memory_space=pltpu.VMEM)
        hbm = pl.BlockSpec(memory_space=pl.ANY)
        dma = pltpu.SemaphoreType.DMA
        out, hist_new = pl.pallas_call(
            functools.partial(kernel, layers, streams, per_stream, beats, rows, tb, pairs),
            out_shape=(
                jax.ShapeDtypeStruct((rows, width), jnp.float32),
                jax.ShapeDtypeStruct((slots * nb, tb, width), jnp.bfloat16),
            ),
            in_specs=[smem] * 5 + [hbm, hbm, hbm, hbm, vmem, vmem, vmem, vmem],
            out_specs=(vmem, vmem),
            scratch_shapes=[
                pltpu.VMEM(((slots + beats * streams) * nb, tb, width), jnp.bfloat16),
                pltpu.VMEM((per_stream * n_tiles + 1, tb, tb), jnp.bfloat16),
                pltpu.VMEM((beats, streams, rows, width), jnp.bfloat16),
                pltpu.VMEM((rows, width), jnp.float32),
                pltpu.VMEM((pairs + 1, tb, width), jnp.bfloat16),
                pltpu.VMEM((rows, width), jnp.bfloat16),
                dma,
                dma,
                dma,
                dma((CHUNKS,)),
                dma((beats, CHUNKS)),
                dma((CHUNKS,)),
                dma((beats, CHUNKS)),
                dma((CHUNKS,)),
                dma((beats, CHUNKS)),
                dma((CHUNKS,)),
                dma((beats, CHUNKS)),
            ],
            compiler_params=pltpu.CompilerParams(
                collective_id=0, has_side_effects=True, vmem_limit_bytes=64000000
            ),
        )(
            *tabs,
            act[0, 0],
            feed[0],
            tiles.reshape(per_stream * n_tiles, tb, tb),
            hist[0].reshape(slots * nb, tb, width),
            mix[0],
            gain,
            up[0],
            down[0],
        )
        return out[None, None], hist_new.reshape(1, slots * rows, width)

    return jax.shard_map(
        local,
        mesh=mesh,
        in_specs=(
            P("layer", "group", None, None),
            P("group", None, None, None),
            P(),
            P(),
            P("group", None, None, None),
            P("group", None),
            P("group", None),
            P("layer", None, None),
            P("layer", None, None),
            P("layer", None),
            P("layer", None, None),
            P("layer", None, None),
        ),
        out_specs=(P("layer", "group", None, None), P("layer", None, None)),
        check_vma=False,
    )
```

```python
import functools

import jax
import jax.numpy as jnp
from jax import lax
from jax.experimental import pallas as pl
from jax.experimental.pallas import tpu as pltpu
from jax.sharding import PartitionSpec as P

MESH = pl.DeviceIdType.MESH
UNROLL = 4


def cuts(nb):
    return [2] * (nb // 2) + [1] * (nb % 2)


def pair_count(tiles, nb):
    pairs = (tiles + nb) // 2
    return -(-pairs // UNROLL) * UNROLL


def kernel(
    layers, streams, per_stream, beats, rows, tb, pairs,
    code, tpos, apos,
    act_ref, feed_ref, tile_ref, hist_ref, mix_ref, gain_ref, up_ref, down_ref,
    out_ref, all_ref, cur_ref,
    hist, tiles, land, stage, segs, sbuf,
    tile_of, block_of, keep_of, last_of, cur,
    local_sem, hist_sem, tile_sem, old_sem, new_sem, y_send, y_recv, sib_send, sib_recv, x_send, x_recv, r_send, r_recv,
):
    layer = lax.axis_index("layer")
    me = lax.axis_index("group")
    core = lax.rem(me, 2)
    sib = me + 1 - 2 * core
    cross = lax.rem(me + 2, streams)
    cross_sib = cross + 1 - 2 * core
    nb = rows // tb
    sizes = cuts(nb)
    chunks = len(sizes)
    starts = [sum(sizes[:k]) for k in range(chunks)]
    slots = streams * per_stream
    first_layer = layer == 0
    last_layer = layer == layers - 1

    old = pltpu.make_async_copy(hist_ref, hist.at[pl.ds(0, slots * nb)], hist_sem)
    old.start()
    load = pltpu.make_async_copy(tile_ref, tiles.at[pl.ds(0, tile_ref.shape[0])], tile_sem)
    load.start()
    tiles[tile_ref.shape[0]] = jnp.zeros((tb, tb), jnp.bfloat16)
    segs[pairs] = jnp.zeros((tb, hist.shape[2]), jnp.bfloat16)

    barrier = pltpu.get_barrier_semaphore()
    for peer in (sib, cross):
        pl.semaphore_signal(barrier, inc=1, device_id={"group": peer}, device_id_type=MESH)

    @pl.when(layer > 0)
    def _():
        pl.semaphore_signal(barrier, inc=1, device_id={"layer": layer - 1}, device_id_type=MESH)

    @pl.when(layer < layers - 1)
    def _():
        pl.semaphore_signal(barrier, inc=1, device_id={"layer": layer + 1}, device_id_type=MESH)

    inner = (layer > 0).astype(jnp.int32) + (layer < layers - 1).astype(jnp.int32)
    pl.semaphore_wait(barrier, 2 + inner)

    def piece(k):
        return pl.ds(starts[k] * tb, sizes[k] * tb)

    def y_copy(b, k):
        return pltpu.make_async_remote_copy(
            src_ref=sbuf.at[piece(k)],
            dst_ref=land.at[b, me, piece(k)],
            send_sem=y_send.at[k],
            recv_sem=y_recv.at[b, k],
            device_id={"layer": layer + 1},
            device_id_type=MESH,
        )

    def group_copy(b, k, stream, send, recv, to):
        return pltpu.make_async_remote_copy(
            src_ref=land.at[b, stream, piece(k)],
            dst_ref=land.at[b, stream, piece(k)],
            send_sem=send.at[k],
            recv_sem=recv.at[b, k],
            device_id={"group": to},
            device_id_type=MESH,
        )

    def keep_rows(b, stream, k):
        at = (slots + b * streams + stream) * nb
        for u in range(starts[k], starts[k] + sizes[k]):
            hist[at + u] = land[b, stream, pl.ds(u * tb, tb), :]

    def new_out(b):
        at = pl.ds((slots + b * streams) * nb, streams * nb)
        return pltpu.make_async_copy(hist.at[at], all_ref.at[at], new_sem.at[b])

    old_at = pl.ds(0, slots * nb)
    old_out = pltpu.make_async_copy(hist.at[old_at], all_ref.at[old_at], old_sem)
    blocks = slots * nb
    wide = 2 * nb

    def decode():
        for j in range(per_stream):
            for k in range(nb):
                last_of[j, k] = pairs

            def one(q, carry):
                for u in range(2):
                    i = 2 * q + u
                    x = code[j, i]
                    rest = lax.div(x, 2 * wide)
                    tile_of[j, i] = lax.div(rest, blocks)
                    block_of[j, i] = lax.rem(rest, blocks)
                x = code[j, 2 * q]
                keep_of[j, q] = 1 - lax.rem(x, 2)
                to = lax.rem(lax.div(x, 2), wide)
                for k in range(nb):
                    last_of[j, k] = jnp.where(to == k, q, last_of[j, k])
                return carry

            lax.fori_loop(0, pairs, one, 0)

    for g in range(slots):
        cur[g] = g

    def slot_of(b, c):
        before = tpos[jnp.maximum(layer - b, 0), c]
        after = apos[c, jnp.maximum(b - 1 - layer, 0)]
        return jnp.where(layer >= b, before, after)

    def beat(b, carry):
        source = jnp.logical_or(b == 0, first_layer)

        @pl.when(b == 0)
        def _():
            c = pltpu.make_async_copy(act_ref, stage, local_sem)
            c.start()
            c.wait()

        @pl.when(jnp.logical_and(b > 0, first_layer))
        def _():
            c = pltpu.make_async_copy(feed_ref.at[jnp.maximum(b - 1, 0)], stage, local_sem)
            c.start()
            c.wait()

        def cross_in(k):
            group_copy(b, k, cross, x_send, x_recv, cross).wait_recv()
            group_copy(b, k, cross, r_send, r_recv, sib).start()
            keep_rows(b, cross, k)

        def sib_in(k):
            group_copy(b, k, sib, sib_send, sib_recv, sib).wait_recv()
            keep_rows(b, sib, k)

        def far_in(k):
            group_copy(b, k, cross_sib, r_send, r_recv, sib).wait_recv()
            keep_rows(b, cross_sib, k)

        for k in range(chunks):
            @pl.when(source)
            def _():
                land[b, me, piece(k), :] = stage[piece(k), :].astype(jnp.bfloat16)

            @pl.when(jnp.logical_not(source))
            def _():
                y_copy(b, k).wait_recv()

            group_copy(b, k, me, x_send, x_recv, cross).start()
            group_copy(b, k, me, sib_send, sib_recv, sib).start()
            keep_rows(b, me, k)
            if k == min(1, chunks - 1):
                @pl.when(b == 0)
                def _():
                    decode()
            if k > 0:
                cross_in(k - 1)
                sib_in(k - 1)
            if k > 1:
                far_in(k - 2)
        sib_in(chunks - 1)
        if chunks > 1:
            far_in(chunks - 2)
        for c in range(streams):
            new = slot_of(b, c)
            for j in range(per_stream):
                g = c * per_stream + j
                cur[g] = jnp.where(new == j, slots + b * streams + c, cur[g])
        own = slot_of(b, me)
        cross_in(chunks - 1)
        far_in(chunks - 1)
        new_out(b).start()

        @pl.when(b == 0)
        def _():
            old.wait()
            load.wait()
            old_out.start()

        def one_pair(q, total):
            def half(h):
                i = 2 * q + h
                block = block_of[own, i]
                at = cur[lax.div(block, nb)] * nb + lax.rem(block, nb)
                return tiles[tile_of[own, i]], hist[at]

            t0, b0 = half(0)
            t1, b1 = half(1)
            product = jnp.dot(
                jnp.concatenate([t0, t1], axis=1),
                jnp.concatenate([b0, b1], axis=0),
                preferred_element_type=jnp.float32,
            )
            total = total * keep_of[own, q].astype(jnp.float32) + product
            segs[q] = total.astype(jnp.bfloat16)
            return total

        def pair_step(s, total):
            for u in range(UNROLL):
                total = one_pair(s * UNROLL + u, total)
            return total

        width = hist.shape[2]
        lax.fori_loop(0, pairs // UNROLL, pair_step, jnp.zeros((tb, width), jnp.float32))

        def rows_step(k):
            blocks = []
            for u in range(starts[k], starts[k] + sizes[k]):
                blocks.append(segs[last_of[own, u]])
            agg = jnp.concatenate(blocks, axis=0) if len(blocks) > 1 else blocks[0]
            act = land[b, me, piece(k), :].astype(jnp.float32)
            mixed = act + jnp.maximum(
                jnp.dot(agg, mix_ref[...], preferred_element_type=jnp.float32), 0.0
            )
            scale = lax.rsqrt(jnp.mean(mixed * mixed, axis=-1, keepdims=True) + 1e-06)
            normed = (mixed * scale * gain_ref[...]).astype(jnp.bfloat16)
            hidden = jax.nn.gelu(
                jnp.dot(normed, up_ref[...], preferred_element_type=jnp.float32)
            ).astype(jnp.bfloat16)
            return mixed + jnp.dot(hidden, down_ref[...], preferred_element_type=jnp.float32)

        sends = jnp.logical_and(b < beats - 1, layer < layers - 1)
        for k in range(chunks):
            @pl.when(jnp.logical_and(b > 0, layer < layers - 1))
            def _():
                y_copy(b, k).wait_send()

            res = rows_step(k)

            @pl.when(b == beats - 1)
            def _():
                out_ref[piece(k), :] = res

            @pl.when(sends)
            def _():
                sbuf[piece(k), :] = res.astype(jnp.bfloat16)
                y_copy(b + 1, k).start()

        for k in range(chunks):
            group_copy(b, k, me, x_send, x_recv, cross).wait_send()
            group_copy(b, k, me, sib_send, sib_recv, sib).wait_send()
            group_copy(b, k, cross, r_send, r_recv, sib).wait_send()
        return carry

    lax.fori_loop(0, beats, beat, 0)

    for g in range(slots):
        cur_ref[g] = cur[g]
    old_out.wait()

    def drain(b, carry):
        new_out(b).wait()
        return carry

    lax.fori_loop(0, beats, drain, 0)


def settle(slots, nb, cur, out_ref, all_ref, res_ref, hist_ref, mid, tmp, in_sem, out_sem):
    def load(g):
        at = pl.ds(cur[g] * nb, nb)
        return pltpu.make_async_copy(all_ref.at[at], mid.at[pl.ds(g * nb, nb)], in_sem.at[g])

    def save(g):
        at = pl.ds(g * nb, nb)
        return pltpu.make_async_copy(mid.at[at], hist_ref.at[at], out_sem.at[g])

    first = pltpu.make_async_copy(out_ref, tmp, in_sem.at[slots])
    second = pltpu.make_async_copy(tmp, res_ref, out_sem.at[slots])
    first.start()
    for g in range(slots):
        load(g).start()
    first.wait()
    second.start()
    for g in range(slots):
        load(g).wait()
        save(g).start()
    for g in range(slots):
        save(g).wait()
    second.wait()


def tables(read, write, nb, blocks):
    per_stream, tiles = read.shape
    pairs = pair_count(tiles, nb)
    i32 = jnp.int32
    js = jnp.arange(per_stream, dtype=i32)
    ks = jnp.arange(nb, dtype=i32)
    ts = jnp.arange(tiles, dtype=i32)
    count = jnp.sum((write[:, None, :] == ks[None, :, None]).astype(i32), axis=2)
    half = (count + 1) // 2
    start = jnp.sum(jnp.where(write[:, :, None] > ks, half[:, None, :], 0), axis=2)
    rank = jnp.sum(
        ((write[:, :, None] == write[:, None, :]) & (ts[None, None, :] < ts[None, :, None])).astype(i32),
        axis=2,
    )
    place = 2 * start + rank
    tile = js[:, None] * tiles + ts
    word = ((tile * blocks + read) * (2 * nb) + write) * 2 + (rank == 0).astype(i32)
    pad = ((per_stream * tiles * blocks) * (2 * nb) + nb) * 2
    qs = jnp.arange(2 * pairs, dtype=i32)
    at = place[:, None, :] == qs[None, :, None]
    return pad + jnp.sum(jnp.where(at, (word - pad)[:, None, :], 0), axis=2)


def solution(mesh):
    layers = mesh.shape["layer"]
    streams = mesh.shape["group"]

    def local(act, feed, tpos, apos, tiles, read, write, hist, mix, gain, up, down):
        rows, width = act.shape[2:]
        per_stream, n_tiles, tb = tiles.shape[:3]
        beats = feed.shape[1]
        nb = rows // tb
        slots = streams * per_stream
        pairs = pair_count(n_tiles, nb)
        chunks = len(cuts(nb))
        total = (slots + beats * streams) * nb
        smem = pl.BlockSpec(memory_space=pltpu.SMEM)
        vmem = pl.BlockSpec(memory_space=pltpu.VMEM)
        hbm = pl.BlockSpec(memory_space=pl.ANY)
        dma = pltpu.SemaphoreType.DMA
        out, everything, cur = pl.pallas_call(
            functools.partial(kernel, layers, streams, per_stream, beats, rows, tb, pairs),
            out_shape=(
                jax.ShapeDtypeStruct((rows, width), jnp.float32),
                jax.ShapeDtypeStruct((total, tb, width), jnp.bfloat16),
                jax.ShapeDtypeStruct((slots,), jnp.int32),
            ),
            in_specs=[smem] * 3 + [hbm, hbm, hbm, hbm, vmem, vmem, vmem, vmem],
            out_specs=(vmem, hbm, smem),
            scratch_shapes=[
                pltpu.VMEM((total, tb, width), jnp.bfloat16),
                pltpu.VMEM((per_stream * n_tiles + 1, tb, tb), jnp.bfloat16),
                pltpu.VMEM((beats, streams, rows, width), jnp.bfloat16),
                pltpu.VMEM((rows, width), jnp.float32),
                pltpu.VMEM((pairs + 1, tb, width), jnp.bfloat16),
                pltpu.VMEM((rows, width), jnp.bfloat16),
                pltpu.SMEM((per_stream, 2 * pairs), jnp.int32),
                pltpu.SMEM((per_stream, 2 * pairs), jnp.int32),
                pltpu.SMEM((per_stream, pairs), jnp.int32),
                pltpu.SMEM((per_stream, nb), jnp.int32),
                pltpu.SMEM((slots,), jnp.int32),
                dma,
                dma,
                dma,
                dma,
                dma((beats,)),
                dma((chunks,)),
                dma((beats, chunks)),
                dma((chunks,)),
                dma((beats, chunks)),
                dma((chunks,)),
                dma((beats, chunks)),
                dma((chunks,)),
                dma((beats, chunks)),
            ],
            compiler_params=pltpu.CompilerParams(
                collective_id=0, has_side_effects=True, vmem_limit_bytes=64000000
            ),
        )(
            tables(read, write, nb, slots * nb),
            tpos,
            apos,
            act[0, 0],
            feed[0],
            tiles.reshape(per_stream * n_tiles, tb, tb),
            hist[0].reshape(slots * nb, tb, width),
            mix[0],
            gain,
            up[0],
            down[0],
        )
        res, hist_new = pl.pallas_call(
            functools.partial(settle, slots, nb),
            out_shape=(
                jax.ShapeDtypeStruct((rows, width), jnp.float32),
                jax.ShapeDtypeStruct((slots * nb, tb, width), jnp.bfloat16),
            ),
            in_specs=[smem, hbm, hbm],
            out_specs=(hbm, hbm),
            scratch_shapes=[
                pltpu.VMEM((slots * nb, tb, width), jnp.bfloat16),
                pltpu.VMEM((rows, width), jnp.float32),
                dma((slots + 1,)),
                dma((slots + 1,)),
            ],
        )(cur, out, everything)
        return res[None, None], hist_new.reshape(1, slots * rows, width)

    return jax.shard_map(
        local,
        mesh=mesh,
        in_specs=(
            P("layer", "group", None, None),
            P("group", None, None, None),
            P(),
            P(),
            P("group", None, None, None),
            P("group", None),
            P("group", None),
            P("layer", None, None),
            P("layer", None, None),
            P("layer", None),
            P("layer", None, None),
            P("layer", None, None),
        ),
        out_specs=(P("layer", "group", None, None), P("layer", None, None)),
        check_vma=False,
    )
```
